512 devices in a mesh: narrow: 16 (over z, core), wide: 32 (over x, y).
Axes of the slice: x: 4, y: 8, z: 8, core: 2. Of those that a mesh axis runs over, the one named last changes fastest.
Arguments:
- field: float32 [128, 512, 1024], P('narrow', 'wide'), may hold values from -12 to 12
- start_block: float32 [1024, 128], replicated, may hold values from -6 to 6
Outputs:
- mode2_gram: float32 [128, 128], P('narrow', 'wide')
The draws below stay inside these ranges and needn't reach their ends.
All inputs are finite; a program needn't handle non-finite values.
Results may differ from the reference program's by a relative error of at most 0.0001.
Values sent between devices are 32-bit elements; how exact they have to be, the bound alone decides.
A program may use at most 64 MiB of HBM per device.

```python
import math
import jax
import jax.numpy as jnp
from jax import lax

I1 = 1024
RANK = 128
ITERS = 4
I2 = 128
I3 = 512


def draw_field(key, part):
    subkeys = jax.random.split(key, 8)
    noise_cells = jnp.clip(jax.random.normal(subkeys[0], (I2, I3, I1), jnp.float32), -4.0, 4.0)
    row_scale = jnp.exp(jax.random.uniform(subkeys[1], (1, 1, I1), jnp.float32, math.log(0.4), math.log(2.5)))
    middle_scale = jnp.exp(jax.random.uniform(subkeys[2], (I2, 1, 1), jnp.float32, math.log(0.6), math.log(1.6)))
    column_scale = jnp.exp(jax.random.uniform(subkeys[3], (1, I3, 1), jnp.float32, math.log(0.3), math.log(3.0)))
    mixing = jnp.eye(I1, dtype=jnp.float32) + 0.7 * jax.random.normal(subkeys[4], (I1, I1), jnp.float32) / math.sqrt(I1)
    mode_two_mix = jnp.eye(I2, dtype=jnp.float32) + jax.random.normal(subkeys[5], (I2, I2), jnp.float32) / math.sqrt(I2)
    scaled = noise_cells * row_scale * column_scale
    blended = jnp.dot(mode_two_mix, scaled.reshape(I2, I3 * I1), precision=lax.Precision.HIGHEST).reshape(I2, I3, I1)
    positions = jnp.arange(I2).astype(jnp.float32)
    phase = jax.random.uniform(subkeys[6], (), jnp.float32, 0.0, 2.0 * math.pi)
    profile = 1.0 + 0.5 * jnp.sin(4.0 * math.pi * positions / I2 + phase)
    shared = jnp.clip(jax.random.normal(subkeys[7], (1, I3, I1), jnp.float32), -4.0, 4.0) * row_scale * column_scale
    combined = (blended + 0.6 * profile.reshape(I2, 1, 1) * shared) * middle_scale
    mixed_field = jnp.dot(combined.reshape(I2 * I3, I1), mixing.T, precision=lax.Precision.HIGHEST)
    return jnp.clip(mixed_field.reshape(I2, I3, I1), -12.0, 12.0)


def centred(rng, extent, deviation, reach, held_as=jnp.bfloat16):
    array = deviation * jax.random.normal(rng, extent, jnp.float32)
    return jnp.clip(array, min=-reach, max=reach).astype(held_as)


def setup_inputs(seed: int = 0) -> dict:
    key_list = jax.random.split(jax.random.key(seed), 3)
    return {
        "field": draw_field(jax.random.fold_in(key_list[2], 71), 0),
        "start_block": centred(key_list[1], (I1, RANK), 1.0, 6.0, jnp.float32),
    }


def orthonormal(vectors):
    inner_gram = jnp.dot(vectors.T, vectors, precision=lax.Precision.HIGHEST)
    factor = jnp.linalg.cholesky(inner_gram)
    return jax.scipy.linalg.solve_triangular(factor, vectors.T, lower=True).T

def reference(field, start_block):
    unfolded = field.reshape(I2 * I3, I1)
    gram_one = jnp.dot(unfolded.T, unfolded, precision=lax.Precision.HIGHEST)
    subspace = orthonormal(start_block)
    for sweep_index in range(ITERS):
        subspace = orthonormal(jnp.dot(gram_one, subspace, precision=lax.Precision.HIGHEST))
    core_cells = jnp.dot(unfolded, subspace, precision=lax.Precision.HIGHEST)
    merged = core_cells.reshape(I2, I3 * RANK)
    product = jnp.dot(merged, merged.T, precision=lax.Precision.HIGHEST)
    return product / (RANK * I3)
```

```python
import jax
import jax.numpy as jnp
from jax import lax
from jax.experimental import pallas as pl
from jax.experimental.pallas import tpu as pltpu
from jax.sharding import PartitionSpec as P

RANK = 128
B3 = 16
ITERS = 4
ROWS = 8
LANES = 128
HIGHEST = lax.Precision.HIGHEST


def lane_copy(block, lane):
    return jnp.broadcast_to(block[:, lane:lane + 1], (ROWS, LANES))


def row_copy(block, row):
    return jnp.broadcast_to(block[row:row + 1, :], (ROWS, LANES))


def tree_sum(terms):
    terms = list(terms)
    while len(terms) > 1:
        terms = [sum(terms[i:i + 2][1:], terms[i]) for i in range(0, len(terms), 2)]
    return terms[0]


def inverse_factor(gram):
    row = lax.broadcasted_iota(jnp.int32, (ROWS, LANES), 0)
    lane = lax.broadcasted_iota(jnp.int32, (ROWS, LANES), 1)
    panels = RANK // ROWS
    left = [gram[ROWS * p:ROWS * (p + 1), :] for p in range(panels)]
    right = [jnp.where(lane == row + ROWS * p, 1.0, 0.0) for p in range(panels)]
    finished = []
    for p in range(panels):
        diag = [lane_copy(left[p], ROWS * p + c) for c in range(ROWS)]
        scaled = [jnp.zeros((ROWS, LANES), jnp.float32) for _ in range(ROWS)]
        for j in range(ROWS):
            pivot = row_copy(diag[j], j)
            inverse = 1.0 / pivot
            root = lax.rsqrt(pivot)
            at_pivot = row == j
            for c in range(j):
                scaled[c] = jnp.where(at_pivot, diag[c] * root, scaled[c])
            scaled[j] = jnp.where(at_pivot, root, scaled[j])
            column = diag[j]
            for c in range(ROWS):
                if c != j:
                    across = row_copy(diag[c], j) * inverse
                    diag[c] = jnp.where(at_pivot, across, diag[c] - column * across)
            diag[j] = jnp.where(at_pivot, inverse, -column * inverse)
        solved_left = tree_sum(diag[c] * row_copy(left[p], c) for c in range(ROWS))
        solved_right = tree_sum(diag[c] * row_copy(right[p], c) for c in range(ROWS))
        finished.append(tree_sum(scaled[c] * row_copy(right[p], c) for c in range(ROWS)))
        left_rows = [row_copy(solved_left, c) for c in range(ROWS)]
        right_rows = [row_copy(solved_right, c) for c in range(ROWS)]
        for q in range(p + 1, panels):
            factors = [lane_copy(left[q], ROWS * p + c) for c in range(ROWS)]
            left[q] = left[q] - tree_sum(factors[c] * left_rows[c] for c in range(ROWS))
            right[q] = right[q] - tree_sum(factors[c] * right_rows[c] for c in range(ROWS))
    return jnp.concatenate(finished, axis=0)


def product(left, right):
    return lax.dot_general(left, right, (((1,), (0,)), ((), ())), precision=HIGHEST,
                           preferred_element_type=jnp.float32)


def product_of_rows(left, right):
    return lax.dot_general(left, right, (((1,), (1,)), ((), ())), precision=HIGHEST,
                           preferred_element_type=jnp.float32)


def orthonormal_kernel(rows_ref, out_ref):
    rows = rows_ref[...]
    out_ref[...] = product(inverse_factor(product_of_rows(rows, rows)), rows)


def iteration_kernel(gram_ref, rows_ref, field_ref, core_ref, current):
    current[...] = product(rows_ref[...], gram_ref[...])

    def sweep(index, carry):
        rows = current[...]
        factor = inverse_factor(product_of_rows(rows, rows))
        current[...] = product(factor, product(rows, gram_ref[...]))
        return carry

    lax.fori_loop(0, ITERS - 1, sweep, 0)
    rows = current[...]
    subspace = product(inverse_factor(product_of_rows(rows, rows)), rows)
    core_ref[...] = product_of_rows(field_ref[...], subspace)


VMEM = pl.BlockSpec(memory_space=pltpu.VMEM)


def transposed_product(left, right):
    return lax.dot_general(left, right, (((0,), (0,)), ((), ())), precision=HIGHEST)


def shards(field, start_block):
    cells_two, cells_three, order_one = field.shape
    unfolded = field.reshape(cells_two * cells_three, order_one)
    start_rows = pl.pallas_call(
        orthonormal_kernel,
        out_shape=jax.ShapeDtypeStruct((RANK, order_one), jnp.float32),
        in_specs=[VMEM],
        out_specs=VMEM,
    )(start_block.T)
    gram_local = transposed_product(unfolded, unfolded)
    gram_whole = lax.psum(gram_local, ("narrow", "wide"))
    core_cells = pl.pallas_call(
        iteration_kernel,
        out_shape=jax.ShapeDtypeStruct((cells_two * cells_three, RANK), jnp.float32),
        in_specs=[VMEM, VMEM, VMEM],
        out_specs=VMEM,
        scratch_shapes=[pltpu.VMEM((RANK, order_one), jnp.float32)],
        compiler_params=pltpu.CompilerParams(vmem_limit_bytes=48 << 20),
    )(gram_whole, start_rows, unfolded)
    core_block = core_cells.reshape(cells_two, cells_three, RANK)
    regrouped = lax.all_to_all(core_block, "narrow", split_axis=2, concat_axis=0, tiled=True)
    merged = regrouped.reshape(regrouped.shape[0], regrouped.shape[1] * regrouped.shape[2])
    gram_part = jnp.dot(merged, merged.T, precision=HIGHEST)
    sectioned = lax.psum_scatter(gram_part, "narrow", scatter_dimension=0, tiled=True)
    finished = lax.psum_scatter(sectioned, "wide", scatter_dimension=1, tiled=True)
    return finished / (RANK * B3 * lax.axis_size("wide"))


def solution(mesh):
    return jax.shard_map(
        shards,
        mesh=mesh,
        in_specs=(P("narrow", "wide", None), P()),
        out_specs=P("narrow", "wide"),
        check_vma=False,
    )
```

```python
import functools

import jax
import jax.numpy as jnp
from jax import lax
from jax.experimental import pallas as pl
from jax.experimental.pallas import tpu as pltpu
from jax.sharding import PartitionSpec as P

RANK = 128
B3 = 16
ITERS = 4
ROWS = 8
LANES = 128
HIGHEST = lax.Precision.HIGHEST
MESH_ID = pl.DeviceIdType.MESH

CORES = 2
CHIPS_Y = 8

TILE = 256
TILE_ROWS = TILE * TILE // LANES
TILES = (((0, 0), (0, 1), (0, 2), (0, 3), (1, 1)), ((1, 2), (1, 3), (2, 2), (2, 3), (3, 3)))
HALF_ROWS = TILE_ROWS * len(TILES[0])

GROUPS = (("zyx", (0, 1)), ("yzx", (2, 3)), ("xyz", (4,)))


def lane_copy(block, lane):
    return jnp.broadcast_to(block[:, lane:lane + 1], (ROWS, LANES))


def row_copy(block, row):
    return jnp.broadcast_to(block[row:row + 1, :], (ROWS, LANES))


def tree_sum(terms):
    terms = list(terms)
    while len(terms) > 1:
        terms = [sum(terms[i:i + 2][1:], terms[i]) for i in range(0, len(terms), 2)]
    return terms[0]


def inverse_factor(gram):
    row = lax.broadcasted_iota(jnp.int32, (ROWS, LANES), 0)
    lane = lax.broadcasted_iota(jnp.int32, (ROWS, LANES), 1)
    panels = RANK // ROWS
    left = [gram[ROWS * p:ROWS * (p + 1), :] for p in range(panels)]
    right = [jnp.where(lane == row + ROWS * p, 1.0, 0.0) for p in range(panels)]
    finished = []
    for p in range(panels):
        diag = [lane_copy(left[p], ROWS * p + c) for c in range(ROWS)]
        scaled = [jnp.zeros((ROWS, LANES), jnp.float32) for _ in range(ROWS)]
        for j in range(ROWS):
            pivot = row_copy(diag[j], j)
            inverse = 1.0 / pivot
            root = lax.rsqrt(pivot)
            at_pivot = row == j
            for c in range(j):
                scaled[c] = jnp.where(at_pivot, diag[c] * root, scaled[c])
            scaled[j] = jnp.where(at_pivot, root, scaled[j])
            column = diag[j]
            for c in range(ROWS):
                if c != j:
                    across = row_copy(diag[c], j) * inverse
                    diag[c] = jnp.where(at_pivot, across, diag[c] - column * across)
            diag[j] = jnp.where(at_pivot, inverse, -column * inverse)
        solved_left = tree_sum(diag[c] * row_copy(left[p], c) for c in range(ROWS))
        solved_right = tree_sum(diag[c] * row_copy(right[p], c) for c in range(ROWS))
        finished.append(tree_sum(scaled[c] * row_copy(right[p], c) for c in range(ROWS)))
        left_rows = [row_copy(solved_left, c) for c in range(ROWS)]
        right_rows = [row_copy(solved_right, c) for c in range(ROWS)]
        for q in range(p + 1, panels):
            factors = [lane_copy(left[q], ROWS * p + c) for c in range(ROWS)]
            left[q] = left[q] - tree_sum(factors[c] * left_rows[c] for c in range(ROWS))
            right[q] = right[q] - tree_sum(factors[c] * right_rows[c] for c in range(ROWS))
    return jnp.concatenate(finished, axis=0)


def product(left, right):
    return lax.dot_general(left, right, (((1,), (0,)), ((), ())), precision=HIGHEST,
                           preferred_element_type=jnp.float32)


def product_of_rows(left, right):
    return lax.dot_general(left, right, (((1,), (1,)), ((), ())), precision=HIGHEST,
                           preferred_element_type=jnp.float32)


def product_of_columns(left, right):
    return lax.dot_general(left.T, right, (((1,), (0,)), ((), ())), precision=HIGHEST,
                           preferred_element_type=jnp.float32)


class Place:
    def __init__(self, chips):
        self.chips = chips
        self.narrow, self.wide = lax.axis_index("narrow"), lax.axis_index("wide")
        self.core = self.narrow % CORES
        self.at = {"z": self.narrow // CORES, "y": self.wide % chips["y"], "x": self.wide // chips["y"]}

    def step(self, axis, offset):
        return (self.at[axis] + offset + self.chips[axis]) % self.chips[axis]

    def device(self, axis, position):
        if axis == "z":
            return (position * CORES + self.core, self.wide)
        if axis == "y":
            return (self.narrow, self.at["x"] * self.chips["y"] + position)
        return (self.narrow, position * self.chips["y"] + self.at["y"])

    def partner(self):
        return (self.narrow + 1 - 2 * self.core, self.wide)

    def along(self, axis):
        return [self.device(axis, self.step(axis, offset)) for offset in range(1, self.chips[axis])]


class Copies:
    def __init__(self, send_sem, recv_sem):
        self.send_sem, self.recv_sem, self.started = send_sem, recv_sem, []

    def start(self, source, target, device):
        index = len(self.started)
        copy = pltpu.make_async_remote_copy(source, target, self.send_sem.at[index], self.recv_sem.at[index],
                                            device_id=device, device_id_type=MESH_ID)
        copy.start()
        self.started.append(copy)
        return copy

    def drain(self):
        for copy in self.started:
            copy.wait_send()


def greet(devices):
    barrier = pltpu.get_barrier_semaphore()
    for device in devices:
        pl.semaphore_signal(barrier, inc=1, device_id=device, device_id_type=MESH_ID)
    pl.semaphore_wait(barrier, len(devices))


def aligned(start, size):
    return pl.ds(pl.multiple_of(start, ROWS), size)


class Group:
    def __init__(self, chips, axes, tiles):
        self.first, self.second, self.third = axes
        self.tiles = tiles
        self.ring = chips[self.first]
        self.ahead, self.behind = self.ring // 2, (self.ring - 1) // 2
        self.block = TILE_ROWS // self.ring
        self.piece = self.block // chips[self.second]
        self.rows = self.piece * len(tiles)
        self.chips = chips

    def scratch(self):
        def rows(*shape):
            return pltpu.VMEM((*shape, LANES), jnp.float32)

        count, second = len(self.tiles), self.chips[self.second]
        return [rows(count, self.ahead, self.block), rows(count, max(self.behind, 1), self.block),
                rows(second, self.rows), rows(max(second - 1, 1), self.rows),
                rows(self.chips[self.third], self.rows), rows(second, self.rows)]

    def copies(self):
        links = len(self.tiles) * (self.ring - 1)
        return 2 * links + 2 * (self.chips[self.second] - 1) + self.chips[self.third] - 1

    def take(self, refs):
        self.up, self.down, self.sums, self.parts, self.slots, self.gathered = refs

    def rows_of(self, tile, position):
        return aligned(tile * TILE_ROWS + position * self.block, self.block)


def gram_kernel(chips, field_ref, out_ref, joined, mine, *rest):
    groups = [Group(chips, axes, tiles) for axes, tiles in GROUPS]
    for number, group in enumerate(groups):
        group.take(rest[6 * number:6 * number + 6])
    copies = Copies(*rest[6 * len(groups):])
    place = Place(chips)
    core = place.core
    greet([place.partner()] + [device for axis in "zyx" for device in place.along(axis)])

    depth = field_ref.shape[0]
    own = aligned(core * depth, depth)
    exchange = copies.start(field_ref, joined.at[own, :], place.partner())
    joined[own, :] = field_ref[...]
    exchange.wait_recv()

    moving = {}

    def send_ahead(group, tile, source, step):
        device = place.device(group.first, place.step(group.first, 1))
        moving[tile, "up", step] = copies.start(source, group.up.at[group.tiles.index(tile), step], device)

    def send_behind(group, tile, source, step):
        device = place.device(group.first, place.step(group.first, -1))
        moving[tile, "down", step] = copies.start(source, group.down.at[group.tiles.index(tile), step], device)

    order = [(group, group.tiles[turn]) for turn in range(2) for group in groups if turn < len(group.tiles)]
    for group, tile in order:
        rows, columns = (TILES[0][tile][side] + core * (TILES[1][tile][side] - TILES[0][tile][side])
                         for side in range(2))
        block = product_of_columns(joined[:, pl.ds(pl.multiple_of(rows * TILE, TILE), TILE)],
                                   joined[:, pl.ds(pl.multiple_of(columns * TILE, TILE), TILE)])
        for half in range(TILE // LANES):
            start = tile * TILE_ROWS + half * TILE
            mine[start:start + TILE, :] = block[:, half * LANES:(half + 1) * LANES]
        send_ahead(group, tile, mine.at[group.rows_of(tile, place.step(group.first, group.ahead)), :], 0)
        if group.behind:
            send_behind(group, tile, mine.at[group.rows_of(tile, place.step(group.first, -group.behind)), :], 0)

    pieces = {}
    for step in range(1, max(group.ahead for group in groups) + 1):
        for group, tile in order:
            index = group.tiles.index(tile)
            if step < group.ahead:
                moving[tile, "up", step - 1].wait_recv()
                target = place.step(group.first, group.ahead - step)
                group.up[index, step - 1] = group.up[index, step - 1] + mine[group.rows_of(tile, target), :]
                send_ahead(group, tile, group.up.at[index, step - 1], step)
            if step < group.behind:
                moving[tile, "down", step - 1].wait_recv()
                target = place.step(group.first, step - group.behind)
                group.down[index, step - 1] = group.down[index, step - 1] + mine[group.rows_of(tile, target), :]
                send_behind(group, tile, group.down.at[index, step - 1], step)
            if step == group.ahead:
                moving[tile, "up", step - 1].wait_recv()
                total = mine[group.rows_of(tile, place.at[group.first]), :] + group.up[index, step - 1]
                if group.behind:
                    moving[tile, "down", group.behind - 1].wait_recv()
                    total = total + group.down[index, group.behind - 1]
                for part in range(chips[group.second]):
                    group.sums[part, index * group.piece:(index + 1) * group.piece, :] = (
                        total[part * group.piece:(part + 1) * group.piece, :])
                if index == len(group.tiles) - 1:
                    pieces[group] = []
                    for offset in range(1, chips[group.second]):
                        to = place.step(group.second, offset)
                        pieces[group].append(copies.start(group.sums.at[to], group.parts.at[offset - 1],
                                                          place.device(group.second, to)))

    arrival = sorted(groups, key=lambda group: group.ahead)
    for group in arrival:
        total = group.sums[place.at[group.second]]
        for number, copy in enumerate(pieces[group]):
            copy.wait_recv()
            total = total + group.parts[number]
        here = place.at[group.third]
        group.slots[here] = total
        pieces[group] = [copies.start(group.slots.at[here], group.slots.at[here], device)
                         for device in place.along(group.third)]
    for group in arrival:
        for copy in pieces[group]:
            copy.wait_recv()
        total = group.slots[0]
        for slot in range(1, chips[group.third]):
            total = total + group.slots[slot]
        here = place.at[group.second]
        group.gathered[here] = total
        pieces[group] = [copies.start(group.gathered.at[here], group.gathered.at[here], device)
                         for device in place.along(group.second)]

    def pass_on(group, tile, way, step):
        sign = 1 if way == "up" else -1
        rows = group.rows_of(tile, place.step(group.first, -sign * step))
        device = place.device(group.first, place.step(group.first, sign))
        moving[tile, way, step] = copies.start(out_ref.at[core, rows, :], out_ref.at[core, rows, :], device)

    for group in arrival:
        for copy in pieces[group]:
            copy.wait_recv()
        for index, tile in enumerate(group.tiles):
            start = tile * TILE_ROWS + place.at[group.first] * group.block
            for part in range(chips[group.second]):
                out_ref[core, aligned(start + part * group.piece, group.piece), :] = (
                    group.gathered[part, index * group.piece:(index + 1) * group.piece, :])
            pass_on(group, tile, "up", 0)
            if group.behind:
                pass_on(group, tile, "down", 0)
    crossing = []
    for step in range(1, max(group.ahead for group in groups) + 1):
        for group, tile in order:
            if step <= group.ahead:
                moving[tile, "up", step - 1].wait_recv()
                if step < group.ahead:
                    pass_on(group, tile, "up", step)
            if step <= group.behind:
                moving[tile, "down", step - 1].wait_recv()
                if step < group.behind:
                    pass_on(group, tile, "down", step)
            if step == group.ahead:
                rows = pl.ds(tile * TILE_ROWS, TILE_ROWS)
                crossing.append(copies.start(out_ref.at[core, rows, :], out_ref.at[core, rows, :], place.partner()))
    for copy in crossing:
        copy.wait_recv()
    copies.drain()


def gram_everywhere(field_rows, chips):
    groups = [Group(chips, axes, tiles) for axes, tiles in GROUPS]
    depth, order = field_rows.shape
    count = 1 + len(TILES[0]) + sum(group.copies() for group in groups)
    return pl.pallas_call(
        functools.partial(gram_kernel, chips),
        out_shape=jax.ShapeDtypeStruct((CORES, HALF_ROWS, LANES), jnp.float32),
        in_specs=[VMEM],
        out_specs=VMEM,
        scratch_shapes=[pltpu.VMEM((CORES * depth, order), jnp.float32), pltpu.VMEM((HALF_ROWS, LANES), jnp.float32)]
        + [shape for group in groups for shape in group.scratch()]
        + [pltpu.SemaphoreType.DMA((count,)), pltpu.SemaphoreType.DMA((count,))],
        compiler_params=pltpu.CompilerParams(collective_id=0, has_side_effects=True, vmem_limit_bytes=48 << 20),
    )(field_rows)


def mode_two_kernel(chips, core_ref, out_ref, leaving, cells, split, terms, rows_y, rows_x, send_sem, recv_sem):
    place, copies = Place(chips), Copies(send_sem, recv_sem)
    devices = CORES * chips["z"]
    others = [(place.narrow + offset) % devices for offset in range(1, devices)]
    greet([(narrow, place.wide) for narrow in others] + place.along("y") + place.along("x"))

    def regroup(source, target):
        target[place.narrow] = source[place.narrow]
        return [copies.start(source.at[narrow], target.at[place.narrow], (narrow, place.wide)) for narrow in others]

    def sum_along(axis, slots, term):
        slots[place.at[axis]] = term
        here = slots.at[place.at[axis]]
        for copy in [copies.start(here, here, device) for device in place.along(axis)]:
            copy.wait_recv()
        return functools.reduce(lambda total, slot: total + slots[slot], range(1, chips[axis]), slots[0])

    for index in range(devices):
        leaving[index] = core_ref[pl.ds(index, ROWS, stride=devices), :]
    for copy in regroup(leaving, cells):
        copy.wait_recv()
    block = cells[...].reshape(devices * ROWS, RANK)
    split[...] = product_of_rows(block, block).reshape(devices, ROWS, devices * ROWS)
    for copy in regroup(split, terms):
        copy.wait_recv()
    total = functools.reduce(lambda total, slot: total + terms[slot], range(1, devices), terms[0])
    total = sum_along("y", rows_y, total)
    out_ref[...] = sum_along("x", rows_x, total)
    copies.drain()


def mode_two_rows(core_cells, chips):
    devices = CORES * chips["z"]
    width = devices * ROWS
    count = 2 * (devices - 1) + chips["y"] + chips["x"] - 2

    def tiles(number, lanes):
        return pltpu.VMEM((number, ROWS, lanes), jnp.float32)

    return pl.pallas_call(
        functools.partial(mode_two_kernel, chips),
        out_shape=jax.ShapeDtypeStruct((ROWS, width), jnp.float32),
        in_specs=[VMEM],
        out_specs=VMEM,
        scratch_shapes=[tiles(devices, RANK), tiles(devices, RANK), tiles(devices, width), tiles(devices, width),
                        tiles(chips["y"], width), tiles(chips["x"], width),
                        pltpu.SemaphoreType.DMA((count,)), pltpu.SemaphoreType.DMA((count,))],
        compiler_params=pltpu.CompilerParams(collective_id=1, has_side_effects=True),
    )(core_cells)


def orthonormal_kernel(rows_ref, out_ref):
    rows = rows_ref[...]
    out_ref[...] = product(inverse_factor(product_of_rows(rows, rows)), rows)


def iteration_kernel(tiles_ref, rows_ref, field_ref, core_ref, gram, current):
    for side in range(CORES):
        for number, (row, column) in enumerate(TILES[side]):
            start = number * TILE_ROWS
            tile = jnp.concatenate([tiles_ref[side, start:start + TILE, :],
                                    tiles_ref[side, start + TILE:start + 2 * TILE, :]], axis=1)
            gram[row * TILE:(row + 1) * TILE, column * TILE:(column + 1) * TILE] = tile
            if row != column:
                gram[column * TILE:(column + 1) * TILE, row * TILE:(row + 1) * TILE] = tile.T
    current[...] = product(rows_ref[...], gram[...])

    def sweep(index, carry):
        rows = current[...]
        factor = inverse_factor(product_of_rows(rows, rows))
        current[...] = product(factor, product(rows, gram[...]))
        return carry

    lax.fori_loop(0, ITERS - 1, sweep, 0)
    rows = current[...]
    subspace = product(inverse_factor(product_of_rows(rows, rows)), rows)
    core_ref[...] = product_of_rows(field_ref[...], subspace)


VMEM = pl.BlockSpec(memory_space=pltpu.VMEM)


def shards(chips, field, start_block):
    cells_two, cells_three, order_one = field.shape
    unfolded = field.reshape(cells_two * cells_three, order_one)
    start_rows = pl.pallas_call(
        orthonormal_kernel,
        out_shape=jax.ShapeDtypeStruct((RANK, order_one), jnp.float32),
        in_specs=[VMEM],
        out_specs=VMEM,
    )(start_block.T)
    gram_tiles = gram_everywhere(unfolded, chips)
    core_cells = pl.pallas_call(
        iteration_kernel,
        out_shape=jax.ShapeDtypeStruct((cells_two * cells_three, RANK), jnp.float32),
        in_specs=[VMEM, VMEM, VMEM],
        out_specs=VMEM,
        scratch_shapes=[pltpu.VMEM((order_one, order_one), jnp.float32), pltpu.VMEM((RANK, order_one), jnp.float32)],
        compiler_params=pltpu.CompilerParams(vmem_limit_bytes=48 << 20),
    )(gram_tiles, start_rows, unfolded)
    rows = mode_two_rows(core_cells, chips)
    columns = rows.shape[1] // lax.axis_size("wide")
    finished = lax.dynamic_slice_in_dim(rows, lax.axis_index("wide") * columns, columns, axis=1)
    return finished / (RANK * B3 * lax.axis_size("wide"))


def solution(mesh, chips_y=CHIPS_Y):
    chips = {"z": mesh.shape["narrow"] // CORES, "y": chips_y, "x": mesh.shape["wide"] // chips_y}
    return jax.shard_map(
        functools.partial(shards, chips),
        mesh=mesh,
        in_specs=(P("narrow", "wide", None), P()),
        out_specs=P("narrow", "wide"),
        check_vma=False,
    )
```

```python
import functools

import jax
import jax.numpy as jnp
from jax import lax
from jax.experimental import pallas as pl
from jax.experimental.pallas import tpu as pltpu
from jax.sharding import PartitionSpec as P

RANK = 128
ITERS = 4
ROWS = 8
LANES = 128
HIGHEST = lax.Precision.HIGHEST
MESH_ID = pl.DeviceIdType.MESH

CORES = 2
CHIPS_Y = 8

TILE = 256
TILE_ROWS = TILE * TILE // LANES
TILES = (((0, 0), (0, 1), (0, 2), (0, 3), (1, 1)), ((1, 2), (1, 3), (2, 2), (2, 3), (3, 3)))
HALF_ROWS = TILE_ROWS * len(TILES[0])

GROUPS = (("zyx", (0, 1)), ("yzx", (2, 3)), ("xyz", (4,)))


def lane_copy(block, lane):
    return jnp.broadcast_to(block[:, lane:lane + 1], (ROWS, LANES))


def row_copy(block, row):
    return jnp.broadcast_to(block[row:row + 1, :], (ROWS, LANES))


def tree_sum(terms):
    terms = list(terms)
    while len(terms) > 1:
        terms = [sum(terms[i:i + 2][1:], terms[i]) for i in range(0, len(terms), 2)]
    return terms[0]


def factor_panels(gram):
    row = lax.broadcasted_iota(jnp.int32, (ROWS, LANES), 0)
    lane = lax.broadcasted_iota(jnp.int32, (ROWS, LANES), 1)
    panels = RANK // ROWS
    left = [gram[ROWS * p:ROWS * (p + 1), :] for p in range(panels)]
    right = [jnp.where(lane == row + ROWS * p, 1.0, 0.0) for p in range(panels)]
    finished = []
    for p in range(panels):
        diag = [jnp.where(row < ROWS, lane_copy(left[p], ROWS * p + c), 0.0) for c in range(ROWS)]
        scaled = [jnp.zeros((ROWS, LANES), jnp.float32) for _ in range(ROWS)]
        for j in range(ROWS):
            pivot = row_copy(diag[j], j)
            inverse = 1.0 / pivot
            root = lax.rsqrt(pivot)
            at_pivot = row == j
            for c in range(j):
                scaled[c] = jnp.where(at_pivot, diag[c] * root, scaled[c])
            scaled[j] = jnp.where(at_pivot, root, scaled[j])
            column = diag[j]
            for c in range(ROWS):
                if c != j:
                    across = row_copy(diag[c], j) * inverse
                    diag[c] = jnp.where(at_pivot, across, diag[c] - column * across)
            diag[j] = jnp.where(at_pivot, inverse, -column * inverse)
        solved_left = tree_sum(diag[c] * row_copy(left[p], c) for c in range(ROWS))
        solved_right = tree_sum(diag[c] * row_copy(right[p], c) for c in range(ROWS))
        finished.append(tree_sum(scaled[c] * row_copy(right[p], c) for c in range(ROWS)))
        left_rows = [row_copy(solved_left, c) for c in range(ROWS)]
        right_rows = [row_copy(solved_right, c) for c in range(ROWS)]
        later = range(p + 1, panels)
        factors = [[lane_copy(left[q], ROWS * p + c) for q in later] for c in range(ROWS)]
        for number, q in enumerate(later):
            left[q] = left[q] - tree_sum(factors[c][number] * left_rows[c] for c in range(ROWS))
            right[q] = right[q] - tree_sum(factors[c][number] * right_rows[c] for c in range(ROWS))
        yield
    return jnp.concatenate(finished, axis=0)


def inverse_factor(gram):
    panels = factor_panels(gram)
    while True:
        try:
            next(panels)
        except StopIteration as stop:
            return stop.value


def product(left, right):
    return lax.dot_general(left, right, (((1,), (0,)), ((), ())), precision=HIGHEST,
                           preferred_element_type=jnp.float32)


def product_of_rows(left, right):
    return lax.dot_general(left, right, (((1,), (1,)), ((), ())), precision=HIGHEST,
                           preferred_element_type=jnp.float32)


def product_of_columns(left, right):
    return lax.dot_general(left.T, right, (((1,), (0,)), ((), ())), precision=HIGHEST,
                           preferred_element_type=jnp.float32)


class Place:
    def __init__(self, chips):
        self.chips = chips
        self.narrow, self.wide = lax.axis_index("narrow"), lax.axis_index("wide")
        self.core = self.narrow % CORES
        self.at = {"z": self.narrow // CORES, "y": self.wide % chips["y"], "x": self.wide // chips["y"]}

    def step(self, axis, offset):
        return (self.at[axis] + offset + self.chips[axis]) % self.chips[axis]

    def device(self, axis, position):
        if axis == "z":
            return (position * CORES + self.core, self.wide)
        if axis == "y":
            return (self.narrow, self.at["x"] * self.chips["y"] + position)
        return (self.narrow, position * self.chips["y"] + self.at["y"])

    def partner(self):
        return (self.narrow + 1 - 2 * self.core, self.wide)

    def along(self, axis):
        return [self.device(axis, self.step(axis, offset)) for offset in range(1, self.chips[axis])]


class Copies:
    def __init__(self, send_sem, recv_sem):
        self.send_sem, self.recv_sem, self.started = send_sem, recv_sem, []

    def start(self, source, target, device):
        index = len(self.started)
        copy = pltpu.make_async_remote_copy(source, target, self.send_sem.at[index], self.recv_sem.at[index],
                                            device_id=device, device_id_type=MESH_ID)
        copy.start()
        self.started.append(copy)
        return copy

    def drain(self):
        for copy in self.started:
            copy.wait_send()


def aligned(start, size):
    return pl.ds(pl.multiple_of(start, ROWS), size)


class Group:
    def __init__(self, chips, axes, tiles):
        self.first, self.second, self.third = axes
        self.tiles = tiles
        self.ring = chips[self.first]
        self.ahead, self.behind = self.ring // 2, (self.ring - 1) // 2
        self.block = TILE_ROWS // self.ring
        self.piece = self.block // chips[self.second]
        self.rows = self.piece * len(tiles)
        self.chips = chips

    def scratch(self):
        def rows(*shape):
            return pltpu.VMEM((*shape, LANES), jnp.float32)

        count, second = len(self.tiles), self.chips[self.second]
        return [rows(count, self.ahead, self.block), rows(count, max(self.behind, 1), self.block),
                rows(second, self.rows), rows(max(second - 1, 1), self.rows),
                rows(self.chips[self.third], self.rows), rows(second, self.rows)]

    def copies(self):
        links = len(self.tiles) * (self.ring - 1)
        return 2 * links + 2 * (self.chips[self.second] - 1) + self.chips[self.third] - 1

    def take(self, refs):
        self.up, self.down, self.sums, self.parts, self.slots, self.gathered = refs

    def rows_of(self, tile, position):
        return aligned(tile * TILE_ROWS + position * self.block, self.block)


def start_rows(rows_ref):
    factor = yield from factor_panels(product_of_rows(rows_ref[...], rows_ref[...]))
    rows_ref[...] = product(factor, rows_ref[...])


def hosvd_kernel(chips, field_ref, start_ref, out_ref, joined, mine, tiles_ref, gram, current, leaving, cells, split,
                 terms, rows_y, rows_x, *rest):
    groups = [Group(chips, axes, tiles) for axes, tiles in GROUPS]
    for number, group in enumerate(groups):
        group.take(rest[6 * number:6 * number + 6])
    copies = Copies(*rest[6 * len(groups):])
    place = Place(chips)
    core = place.core
    devices = CORES * chips["z"]
    others = [(place.narrow + offset) % devices for offset in range(1, devices)]

    barrier = pltpu.get_barrier_semaphore()
    greeted = [(narrow, place.wide) for narrow in others] + place.along("y") + place.along("x")
    for device in greeted:
        pl.semaphore_signal(barrier, inc=1, device_id=device, device_id_type=MESH_ID)
    current[...] = start_ref[...].T
    leaving[...] = jnp.swapaxes(field_ref[...].reshape(ROWS, devices, field_ref.shape[1]), 0, 1)
    pl.semaphore_wait(barrier, len(greeted))

    depth = field_ref.shape[0]
    own = aligned(core * depth, depth)
    exchange = copies.start(field_ref, joined.at[own, :], place.partner())
    joined[own, :] = field_ref[...]
    starting = start_rows(current)

    def advance(panels):
        for _ in range(panels):
            next(starting, None)

    advance(1)
    exchange.wait_recv()

    moving = {}

    def send_ahead(group, tile, source, step):
        device = place.device(group.first, place.step(group.first, 1))
        moving[tile, "up", step] = copies.start(source, group.up.at[group.tiles.index(tile), step], device)

    def send_behind(group, tile, source, step):
        device = place.device(group.first, place.step(group.first, -1))
        moving[tile, "down", step] = copies.start(source, group.down.at[group.tiles.index(tile), step], device)

    order = [(group, group.tiles[turn]) for turn in range(2) for group in groups if turn < len(group.tiles)]
    for group, tile in order:
        rows, columns = (TILES[0][tile][side] + core * (TILES[1][tile][side] - TILES[0][tile][side])
                         for side in range(2))
        block = product_of_columns(joined[:, pl.ds(pl.multiple_of(rows * TILE, TILE), TILE)],
                                   joined[:, pl.ds(pl.multiple_of(columns * TILE, TILE), TILE)])
        for half in range(TILE // LANES):
            start = tile * TILE_ROWS + half * TILE
            mine[start:start + TILE, :] = block[:, half * LANES:(half + 1) * LANES]
        send_ahead(group, tile, mine.at[group.rows_of(tile, place.step(group.first, group.ahead)), :], 0)
        if group.behind:
            send_behind(group, tile, mine.at[group.rows_of(tile, place.step(group.first, -group.behind)), :], 0)

    pieces = {}
    for step in range(1, max(group.ahead for group in groups) + 1):
        advance(2)
        for group, tile in order:
            index = group.tiles.index(tile)
            if step < group.ahead:
                moving[tile, "up", step - 1].wait_recv()
                target = place.step(group.first, group.ahead - step)
                group.up[index, step - 1] = group.up[index, step - 1] + mine[group.rows_of(tile, target), :]
                send_ahead(group, tile, group.up.at[index, step - 1], step)
            if step < group.behind:
                moving[tile, "down", step - 1].wait_recv()
                target = place.step(group.first, step - group.behind)
                group.down[index, step - 1] = group.down[index, step - 1] + mine[group.rows_of(tile, target), :]
                send_behind(group, tile, group.down.at[index, step - 1], step)
            if step == group.ahead:
                moving[tile, "up", step - 1].wait_recv()
                total = mine[group.rows_of(tile, place.at[group.first]), :] + group.up[index, step - 1]
                if group.behind:
                    moving[tile, "down", group.behind - 1].wait_recv()
                    total = total + group.down[index, group.behind - 1]
                for part in range(chips[group.second]):
                    group.sums[part, index * group.piece:(index + 1) * group.piece, :] = (
                        total[part * group.piece:(part + 1) * group.piece, :])
                if index == len(group.tiles) - 1:
                    pieces[group] = []
                    for offset in range(1, chips[group.second]):
                        to = place.step(group.second, offset)
                        pieces[group].append(copies.start(group.sums.at[to], group.parts.at[offset - 1],
                                                          place.device(group.second, to)))

    arrival = sorted(groups, key=lambda group: group.ahead)
    advance(3)
    for group in arrival:
        total = group.sums[place.at[group.second]]
        for number, copy in enumerate(pieces[group]):
            copy.wait_recv()
            total = total + group.parts[number]
        here = place.at[group.third]
        group.slots[here] = total
        pieces[group] = [copies.start(group.slots.at[here], group.slots.at[here], device)
                         for device in place.along(group.third)]
    advance(3)
    for group in arrival:
        for copy in pieces[group]:
            copy.wait_recv()
        total = group.slots[0]
        for slot in range(1, chips[group.third]):
            total = total + group.slots[slot]
        here = place.at[group.second]
        group.gathered[here] = total
        pieces[group] = [copies.start(group.gathered.at[here], group.gathered.at[here], device)
                         for device in place.along(group.second)]

    def pass_on(group, tile, way, step):
        sign = 1 if way == "up" else -1
        rows = group.rows_of(tile, place.step(group.first, -sign * step))
        device = place.device(group.first, place.step(group.first, sign))
        moving[tile, way, step] = copies.start(tiles_ref.at[core, rows, :], tiles_ref.at[core, rows, :], device)

    advance(RANK)
    for group in arrival:
        for copy in pieces[group]:
            copy.wait_recv()
        for index, tile in enumerate(group.tiles):
            start = tile * TILE_ROWS + place.at[group.first] * group.block
            for part in range(chips[group.second]):
                tiles_ref[core, aligned(start + part * group.piece, group.piece), :] = (
                    group.gathered[part, index * group.piece:(index + 1) * group.piece, :])
            pass_on(group, tile, "up", 0)
            if group.behind:
                pass_on(group, tile, "down", 0)
    def unpack(side, tile):
        row, column = (pl.multiple_of((TILES[0][tile][way] + side * (TILES[1][tile][way] - TILES[0][tile][way])) * TILE,
                                      TILE) for way in range(2))
        start = tile * TILE_ROWS
        block = jnp.concatenate([tiles_ref[side, start:start + TILE, :],
                                 tiles_ref[side, start + TILE:start + 2 * TILE, :]], axis=1)
        gram[pl.ds(row, TILE), pl.ds(column, TILE)] = block
        gram[pl.ds(column, TILE), pl.ds(row, TILE)] = block.T

    crossing = {}
    for step in range(1, max(group.ahead for group in groups) + 1):
        for group, tile in order:
            if step <= group.ahead:
                moving[tile, "up", step - 1].wait_recv()
                if step < group.ahead:
                    pass_on(group, tile, "up", step)
            if step <= group.behind:
                moving[tile, "down", step - 1].wait_recv()
                if step < group.behind:
                    pass_on(group, tile, "down", step)
            if step == group.ahead:
                rows = pl.ds(tile * TILE_ROWS, TILE_ROWS)
                crossing[tile] = copies.start(tiles_ref.at[core, rows, :], tiles_ref.at[core, rows, :],
                                              place.partner())
                unpack(core, tile)
    for tile, copy in crossing.items():
        copy.wait_recv()
        unpack(1 - core, tile)

    def regroup(source, target):
        target[place.narrow] = source[place.narrow]
        return [copies.start(source.at[narrow], target.at[place.narrow], (narrow, place.wide)) for narrow in others]

    def sum_along(axis, slots, term):
        slots[place.at[axis]] = term
        here = slots.at[place.at[axis]]
        for copy in [copies.start(here, here, device) for device in place.along(axis)]:
            copy.wait_recv()
        return functools.reduce(lambda total, slot: total + slots[slot], range(1, chips[axis]), slots[0])

    arriving = regroup(leaving, cells)
    current[...] = product(current[...], gram[...])

    def sweep(index, carry):
        rows = current[...]
        factor = inverse_factor(product_of_rows(rows, rows))
        current[...] = product(factor, product(rows, gram[...]))
        return carry

    lax.fori_loop(0, ITERS - 1, sweep, 0)
    rows = current[...]
    subspace = product(inverse_factor(product_of_rows(rows, rows)), rows)
    for copy in arriving:
        copy.wait_recv()
    block = product_of_rows(cells[...].reshape(devices * ROWS, cells.shape[2]), subspace)
    split[...] = product_of_rows(block, block).reshape(devices, ROWS, devices * ROWS)
    for copy in regroup(split, terms):
        copy.wait_recv()
    total = functools.reduce(lambda total, slot: total + terms[slot], range(1, devices), terms[0])
    out_ref[...] = sum_along("x", rows_x, sum_along("y", rows_y, total))
    copies.drain()


VMEM = pl.BlockSpec(memory_space=pltpu.VMEM)


def mode_two_rows(field_rows, start_block, chips):
    groups = [Group(chips, axes, tiles) for axes, tiles in GROUPS]
    depth, order = field_rows.shape
    devices = CORES * chips["z"]
    width = devices * ROWS
    count = (1 + len(TILES[0]) + sum(group.copies() for group in groups) + 2 * (devices - 1) + chips["y"] + chips["x"]
             - 2)

    def floats(*shape):
        return pltpu.VMEM(shape, jnp.float32)

    return pl.pallas_call(
        functools.partial(hosvd_kernel, chips),
        out_shape=jax.ShapeDtypeStruct((ROWS, width), jnp.float32),
        in_specs=[VMEM, VMEM],
        out_specs=VMEM,
        scratch_shapes=[floats(CORES * depth, order), floats(HALF_ROWS, LANES), floats(CORES, HALF_ROWS, LANES),
                        floats(order, order), floats(RANK, order), floats(devices, ROWS, order),
                        floats(devices, ROWS, order), floats(devices, ROWS, width), floats(devices, ROWS, width),
                        floats(chips["y"], ROWS, width), floats(chips["x"], ROWS, width)]
        + [shape for group in groups for shape in group.scratch()]
        + [pltpu.SemaphoreType.DMA((count,)), pltpu.SemaphoreType.DMA((count,))],
        compiler_params=pltpu.CompilerParams(collective_id=0, has_side_effects=True, vmem_limit_bytes=48 << 20),
    )(field_rows, start_block)


def shards(chips, field, start_block):
    cells_two, cells_three, order_one = field.shape
    rows = mode_two_rows(field.reshape(cells_two * cells_three, order_one), start_block, chips)
    columns = rows.shape[1] // lax.axis_size("wide")
    finished = lax.dynamic_slice_in_dim(rows, lax.axis_index("wide") * columns, columns, axis=1)
    return finished / (RANK * cells_three * lax.axis_size("wide"))


def solution(mesh, chips_y=CHIPS_Y):
    chips = {"z": mesh.shape["narrow"] // CORES, "y": chips_y, "x": mesh.shape["wide"] // chips_y}
    return jax.shard_map(
        functools.partial(shards, chips),
        mesh=mesh,
        in_specs=(P("narrow", "wide", None), P()),
        out_specs=P("narrow", "wide"),
        check_vma=False,
    )
```

```python
import functools

import jax
import jax.numpy as jnp
from jax import lax
from jax.experimental import pallas as pl
from jax.experimental.pallas import tpu as pltpu
from jax.sharding import PartitionSpec as P

RANK = 128
ITERS = 4
ROWS = 8
LANES = 128
HIGHEST = lax.Precision.HIGHEST
MESH_ID = pl.DeviceIdType.MESH

CORES = 2
CHIPS_Y = 8

TILE = 256
TILE_ROWS = TILE * TILE // LANES
TILES = (((0, 0), (0, 1), (0, 2), (0, 3), (1, 1)), ((1, 2), (1, 3), (2, 2), (2, 3), (3, 3)))
HALF_ROWS = TILE_ROWS * len(TILES[0])

GROUPS = (("zyx", (0, 1)), ("yzx", (2, 3)), ("xyz", (4,)))


def lane_copy(block, lane):
    return jnp.broadcast_to(block[:, lane:lane + 1], (ROWS, LANES))


def row_copy(block, row):
    return jnp.broadcast_to(block[row:row + 1, :], (ROWS, LANES))


def tree_sum(terms):
    terms = list(terms)
    while len(terms) > 1:
        terms = [sum(terms[i:i + 2][1:], terms[i]) for i in range(0, len(terms), 2)]
    return terms[0]


def factor_panels(gram):
    row = lax.broadcasted_iota(jnp.int32, (ROWS, LANES), 0)
    lane = lax.broadcasted_iota(jnp.int32, (ROWS, LANES), 1)
    panels = RANK // ROWS
    left = [gram[ROWS * p:ROWS * (p + 1), :] for p in range(panels)]
    right = [jnp.where(lane == row + ROWS * p, 1.0, 0.0) for p in range(panels)]
    finished = []
    for p in range(panels):
        diag = [jnp.where(row < ROWS, lane_copy(left[p], ROWS * p + c), 0.0) for c in range(ROWS)]
        scaled = [jnp.zeros((ROWS, LANES), jnp.float32) for _ in range(ROWS)]
        for j in range(ROWS):
            pivot = row_copy(diag[j], j)
            inverse = 1.0 / pivot
            root = lax.rsqrt(pivot)
            at_pivot = row == j
            for c in range(j):
                scaled[c] = jnp.where(at_pivot, diag[c] * root, scaled[c])
            scaled[j] = jnp.where(at_pivot, root, scaled[j])
            column = diag[j]
            for c in range(ROWS):
                if c != j:
                    across = row_copy(diag[c], j) * inverse
                    diag[c] = jnp.where(at_pivot, across, diag[c] - column * across)
            diag[j] = jnp.where(at_pivot, inverse, -column * inverse)
        solved_left = tree_sum(diag[c] * row_copy(left[p], c) for c in range(ROWS))
        solved_right = tree_sum(diag[c] * row_copy(right[p], c) for c in range(ROWS))
        finished.append(tree_sum(scaled[c] * row_copy(right[p], c) for c in range(ROWS)))
        left_rows = [row_copy(solved_left, c) for c in range(ROWS)]
        right_rows = [row_copy(solved_right, c) for c in range(ROWS)]
        later = range(p + 1, panels)
        factors = [[lane_copy(left[q], ROWS * p + c) for q in later] for c in range(ROWS)]
        for number, q in enumerate(later):
            left[q] = left[q] - tree_sum(factors[c][number] * left_rows[c] for c in range(ROWS))
            right[q] = right[q] - tree_sum(factors[c][number] * right_rows[c] for c in range(ROWS))
        yield
    return jnp.concatenate(finished, axis=0)


def inverse_factor(gram):
    panels = factor_panels(gram)
    while True:
        try:
            next(panels)
        except StopIteration as stop:
            return stop.value


def product(left, right):
    return lax.dot_general(left, right, (((1,), (0,)), ((), ())), precision=HIGHEST,
                           preferred_element_type=jnp.float32)


def product_of_rows(left, right):
    return lax.dot_general(left, right, (((1,), (1,)), ((), ())), precision=HIGHEST,
                           preferred_element_type=jnp.float32)


def two_terms(values):
    high = values.astype(jnp.bfloat16)
    return high, (values - high.astype(jnp.float32)).astype(jnp.bfloat16)


def term_product(left, right, contract):
    return lax.dot_general(left, right, ((contract, (0,)), ((), ())), preferred_element_type=jnp.float32)


class Place:
    def __init__(self, chips):
        self.chips = chips
        self.narrow, self.wide = lax.axis_index("narrow"), lax.axis_index("wide")
        self.core = self.narrow % CORES
        self.at = {"z": self.narrow // CORES, "y": self.wide % chips["y"], "x": self.wide // chips["y"]}

    def step(self, axis, offset):
        return (self.at[axis] + offset + self.chips[axis]) % self.chips[axis]

    def device(self, axis, position):
        if axis == "z":
            return (position * CORES + self.core, self.wide)
        if axis == "y":
            return (self.narrow, self.at["x"] * self.chips["y"] + position)
        return (self.narrow, position * self.chips["y"] + self.at["y"])

    def partner(self):
        return (self.narrow + 1 - 2 * self.core, self.wide)

    def along(self, axis):
        return [self.device(axis, self.step(axis, offset)) for offset in range(1, self.chips[axis])]


class Copies:
    def __init__(self, send_sem, recv_sem):
        self.send_sem, self.recv_sem, self.started = send_sem, recv_sem, []

    def start(self, source, target, device):
        index = len(self.started)
        copy = pltpu.make_async_remote_copy(source, target, self.send_sem.at[index], self.recv_sem.at[index],
                                            device_id=device, device_id_type=MESH_ID)
        copy.start()
        self.started.append(copy)
        return copy

    def drain(self):
        for copy in self.started:
            copy.wait_send()


def aligned(start, size):
    return pl.ds(pl.multiple_of(start, ROWS), size)


class Group:
    def __init__(self, chips, axes, tiles):
        self.first, self.second, self.third = axes
        self.tiles = tiles
        self.ring = chips[self.first]
        self.ahead, self.behind = self.ring // 2, (self.ring - 1) // 2
        self.block = TILE_ROWS // self.ring
        self.piece = self.block // chips[self.second]
        self.rows = self.piece * len(tiles)
        self.chips = chips

    def scratch(self):
        def rows(*shape):
            return pltpu.VMEM((*shape, LANES), jnp.float32)

        count, second = len(self.tiles), self.chips[self.second]
        return [rows(count, self.ahead, self.block), rows(count, max(self.behind, 1), self.block),
                rows(second, self.rows), rows(max(second - 1, 1), self.rows),
                rows(self.chips[self.third], self.rows), rows(second, self.rows)]

    def copies(self):
        links = len(self.tiles) * (self.ring - 1)
        return 2 * links + len(self.tiles) * self.ring + 2 * (self.chips[self.second] - 1) + self.chips[self.third] - 1

    def take(self, refs):
        self.up, self.down, self.sums, self.parts, self.slots, self.gathered = refs

    def rows_of(self, tile, position):
        return aligned(tile * TILE_ROWS + position * self.block, self.block)


def start_rows(rows_ref):
    factor = yield from factor_panels(product_of_rows(rows_ref[...], rows_ref[...]))
    rows_ref[...] = product(factor, rows_ref[...])


def hosvd_kernel(chips, field_hbm, start_hbm, out_ref, start_ref, joined, joined_terms, mine, tiles_ref, gram, current,
                 ahead, leaving, cells, split, terms, rows_y, rows_x, load_sem, *rest):
    groups = [Group(chips, axes, tiles) for axes, tiles in GROUPS]
    for number, group in enumerate(groups):
        group.take(rest[6 * number:6 * number + 6])
    copies = Copies(*rest[6 * len(groups):])
    place = Place(chips)
    core = place.core
    devices = CORES * chips["z"]
    others = [(place.narrow + offset) % devices for offset in range(1, devices)]

    barrier = pltpu.get_barrier_semaphore()
    greeted = [(narrow, place.wide) for narrow in others] + place.along("y") + place.along("x")
    for device in greeted:
        pl.semaphore_signal(barrier, inc=1, device_id=device, device_id_type=MESH_ID)
    depth, order_one = field_hbm.shape
    own = aligned(core * depth, depth)
    loads = [pltpu.make_async_copy(field_hbm, joined.at[own, :], load_sem.at[0]),
             pltpu.make_async_copy(start_hbm, start_ref, load_sem.at[1])]
    for load in loads:
        load.start()
    loads[0].wait()
    leaving[...] = jnp.swapaxes(joined[own, :].reshape(ROWS, devices, order_one), 0, 1)
    pl.semaphore_wait(barrier, len(greeted))

    exchange = copies.start(joined.at[own, :], joined.at[own, :], place.partner())
    loads[1].wait()
    current[...] = start_ref[...].T
    starting = start_rows(current)

    def advance(panels):
        for _ in range(panels):
            next(starting, None)

    advance(1)
    exchange.wait_recv()
    for number, term in enumerate(two_terms(joined[...])):
        joined_terms[number] = term

    moving = {}

    def send_ahead(group, tile, source, step):
        device = place.device(group.first, place.step(group.first, 1))
        moving[tile, "up", step] = copies.start(source, group.up.at[group.tiles.index(tile), step], device)

    def send_behind(group, tile, source, step):
        device = place.device(group.first, place.step(group.first, -1))
        moving[tile, "down", step] = copies.start(source, group.down.at[group.tiles.index(tile), step], device)

    order = [(group, group.tiles[turn]) for turn in range(2) for group in groups if turn < len(group.tiles)]
    for group, tile in order:
        rows, columns = (TILES[0][tile][side] + core * (TILES[1][tile][side] - TILES[0][tile][side])
                         for side in range(2))
        row_high, row_low, column_high, column_low = (
            joined_terms[number, :, pl.ds(pl.multiple_of(side * TILE, TILE), TILE)]
            for side in (rows, columns) for number in range(2))
        block = term_product(row_high, column_high, (0,)) + (
            term_product(row_high, column_low, (0,)) + term_product(row_low, column_high, (0,)))
        for half in range(TILE // LANES):
            start = tile * TILE_ROWS + half * TILE
            mine[start:start + TILE, :] = block[:, half * LANES:(half + 1) * LANES]
        send_ahead(group, tile, mine.at[group.rows_of(tile, place.step(group.first, group.ahead)), :], 0)
        if group.behind:
            send_behind(group, tile, mine.at[group.rows_of(tile, place.step(group.first, -group.behind)), :], 0)

    pieces = {}
    for step in range(1, max(group.ahead for group in groups) + 1):
        advance(3)
        for group, tile in order:
            index = group.tiles.index(tile)
            if step < group.ahead:
                moving[tile, "up", step - 1].wait_recv()
                target = place.step(group.first, group.ahead - step)
                group.up[index, step - 1] = group.up[index, step - 1] + mine[group.rows_of(tile, target), :]
                send_ahead(group, tile, group.up.at[index, step - 1], step)
            if step < group.behind:
                moving[tile, "down", step - 1].wait_recv()
                target = place.step(group.first, step - group.behind)
                group.down[index, step - 1] = group.down[index, step - 1] + mine[group.rows_of(tile, target), :]
                send_behind(group, tile, group.down.at[index, step - 1], step)
            if step == group.ahead:
                moving[tile, "up", step - 1].wait_recv()
                total = mine[group.rows_of(tile, place.at[group.first]), :] + group.up[index, step - 1]
                if group.behind:
                    moving[tile, "down", group.behind - 1].wait_recv()
                    total = total + group.down[index, group.behind - 1]
                for part in range(chips[group.second]):
                    group.sums[part, index * group.piece:(index + 1) * group.piece, :] = (
                        total[part * group.piece:(part + 1) * group.piece, :])
                if index == len(group.tiles) - 1:
                    pieces[group] = []
                    for offset in range(1, chips[group.second]):
                        to = place.step(group.second, offset)
                        pieces[group].append(copies.start(group.sums.at[to], group.parts.at[offset - 1],
                                                          place.device(group.second, to)))

    arrival = sorted(groups, key=lambda group: group.ahead)
    advance(3)
    for group in arrival:
        total = group.sums[place.at[group.second]]
        for number, copy in enumerate(pieces[group]):
            copy.wait_recv()
            total = total + group.parts[number]
        here = place.at[group.third]
        group.slots[here] = total
        pieces[group] = [copies.start(group.slots.at[here], group.slots.at[here], device)
                         for device in place.along(group.third)]
    advance(RANK)
    for group in arrival:
        for copy in pieces[group]:
            copy.wait_recv()
        total = group.slots[0]
        for slot in range(1, chips[group.third]):
            total = total + group.slots[slot]
        here = place.at[group.second]
        group.gathered[here] = total
        pieces[group] = [copies.start(group.gathered.at[here], group.gathered.at[here], device)
                         for device in place.along(group.second)]

    crossing = {tile: [] for group in groups for tile in group.tiles}

    def cross(tile, rows):
        crossing[tile].append(copies.start(tiles_ref.at[core, rows, :], tiles_ref.at[core, rows, :], place.partner()))

    def pass_on(group, tile, way, step):
        sign = 1 if way == "up" else -1
        rows = group.rows_of(tile, place.step(group.first, -sign * step))
        if way == "up" or step:
            cross(tile, rows)
        if step == (group.ahead if way == "up" else group.behind):
            return
        device = place.device(group.first, place.step(group.first, sign))
        moving[tile, way, step] = copies.start(tiles_ref.at[core, rows, :], tiles_ref.at[core, rows, :], device)

    for group in arrival:
        for copy in pieces[group]:
            copy.wait_recv()
        for index, tile in enumerate(group.tiles):
            start = tile * TILE_ROWS + place.at[group.first] * group.block
            for part in range(chips[group.second]):
                tiles_ref[core, aligned(start + part * group.piece, group.piece), :] = (
                    group.gathered[part, index * group.piece:(index + 1) * group.piece, :])
            pass_on(group, tile, "up", 0)
            if group.behind:
                pass_on(group, tile, "down", 0)
    def unpack(side, tile):
        row, column = (pl.multiple_of((TILES[0][tile][way] + side * (TILES[1][tile][way] - TILES[0][tile][way])) * TILE,
                                      TILE) for way in range(2))
        start = tile * TILE_ROWS
        block = jnp.concatenate([tiles_ref[side, start:start + TILE, :],
                                 tiles_ref[side, start + TILE:start + 2 * TILE, :]], axis=1)
        for number, term in enumerate(two_terms(block)):
            gram[number, pl.ds(row, TILE), pl.ds(column, TILE)] = term
        for number, term in enumerate(two_terms(block.T)):
            gram[number, pl.ds(column, TILE), pl.ds(row, TILE)] = term

    def unpack_across(tile):
        for copy in crossing[tile]:
            copy.wait_recv()
        unpack(1 - core, tile)

    waiting = []
    for step in range(1, max(group.ahead for group in groups) + 1):
        for group, tile in order:
            if step <= group.ahead:
                moving[tile, "up", step - 1].wait_recv()
                pass_on(group, tile, "up", step)
            if step <= group.behind:
                moving[tile, "down", step - 1].wait_recv()
                pass_on(group, tile, "down", step)
        for tile in waiting:
            unpack_across(tile)
        waiting = [tile for group, tile in order if step == group.ahead]
        for tile in waiting:
            unpack(core, tile)
    for tile in waiting:
        unpack_across(tile)

    def regroup(source, target):
        target[place.narrow] = source[place.narrow]
        return [copies.start(source.at[narrow], target.at[place.narrow], (narrow, place.wide)) for narrow in others]

    def sum_along(axis, slots, term):
        slots[place.at[axis]] = term
        here = slots.at[place.at[axis]]
        for copy in [copies.start(here, here, device) for device in place.along(axis)]:
            copy.wait_recv()
        return functools.reduce(lambda total, slot: total + slots[slot], range(1, chips[axis]), slots[0])

    arriving = regroup(leaving, cells)

    def gram_times(rows):
        high, low = two_terms(rows)
        both = term_product(jnp.concatenate([high, low], axis=0), gram[0], (1,))
        ahead[...] = both[:RANK] + (both[RANK:] + term_product(high, gram[1], (1,)))

    gram_times(current[...])
    current[...] = ahead[...]

    def sweep(index, carry):
        rows = current[...]
        factor = inverse_factor(product_of_rows(rows, rows))
        gram_times(rows)
        current[...] = product(factor, ahead[...])
        return carry

    lax.fori_loop(0, ITERS - 1, sweep, 0)
    rows = current[...]
    for copy in arriving:
        copy.wait_recv()
    core_rows = product_of_rows(cells[...].reshape(devices * ROWS, order_one), rows)
    block = product_of_rows(core_rows, inverse_factor(product_of_rows(rows, rows)))
    split[...] = product_of_rows(block, block).reshape(devices, ROWS, devices * ROWS)
    for copy in regroup(split, terms):
        copy.wait_recv()
    total = functools.reduce(lambda total, slot: total + terms[slot], range(1, devices), terms[0])
    out_ref[...] = sum_along("x", rows_x, sum_along("y", rows_y, total))
    copies.drain()


VMEM = pl.BlockSpec(memory_space=pltpu.VMEM)


def mode_two_rows(field_rows, start_block, chips):
    groups = [Group(chips, axes, tiles) for axes, tiles in GROUPS]
    depth, order = field_rows.shape
    devices = CORES * chips["z"]
    width = devices * ROWS
    count = (1 + len(TILES[0]) + sum(group.copies() for group in groups) + 2 * (devices - 1) + chips["y"] + chips["x"]
             - 2)

    def floats(*shape):
        return pltpu.VMEM(shape, jnp.float32)

    def terms(*shape):
        return pltpu.VMEM((2, *shape), jnp.bfloat16)

    return pl.pallas_call(
        functools.partial(hosvd_kernel, chips),
        out_shape=jax.ShapeDtypeStruct((ROWS, width), jnp.float32),
        in_specs=[pl.BlockSpec(memory_space=pl.ANY)] * 2,
        out_specs=VMEM,
        scratch_shapes=[floats(order, RANK), floats(CORES * depth, order), terms(CORES * depth, order),
                        floats(HALF_ROWS, LANES), floats(CORES, HALF_ROWS, LANES), terms(order, order),
                        floats(RANK, order), floats(RANK, order), floats(devices, ROWS, order),
                        floats(devices, ROWS, order), floats(devices, ROWS, width), floats(devices, ROWS, width),
                        floats(chips["y"], ROWS, width), floats(chips["x"], ROWS, width),
                        pltpu.SemaphoreType.DMA((2,))]
        + [shape for group in groups for shape in group.scratch()]
        + [pltpu.SemaphoreType.DMA((count,)), pltpu.SemaphoreType.DMA((count,))],
        compiler_params=pltpu.CompilerParams(collective_id=0, has_side_effects=True, vmem_limit_bytes=48 << 20),
    )(field_rows, start_block)


def shards(chips, field, start_block):
    cells_two, cells_three, order_one = field.shape
    rows = mode_two_rows(field.reshape(cells_two * cells_three, order_one), start_block, chips)
    columns = rows.shape[1] // lax.axis_size("wide")
    finished = lax.dynamic_slice_in_dim(rows, lax.axis_index("wide") * columns, columns, axis=1)
    return finished / (RANK * cells_three * lax.axis_size("wide"))


def solution(mesh, chips_y=CHIPS_Y):
    chips = {"z": mesh.shape["narrow"] // CORES, "y": chips_y, "x": mesh.shape["wide"] // chips_y}
    return jax.shard_map(
        functools.partial(shards, chips),
        mesh=mesh,
        in_specs=(P("narrow", "wide", None), P()),
        out_specs=P("narrow", "wide"),
        check_vma=False,
    )
```

```python
import functools

import jax
import jax.numpy as jnp
from jax import lax
from jax.experimental import pallas as pl
from jax.experimental.pallas import tpu as pltpu
from jax.sharding import PartitionSpec as P

RANK = 128
ITERS = 4
ROWS = 8
LANES = 128
HIGHEST = lax.Precision.HIGHEST
MESH_ID = pl.DeviceIdType.MESH

CORES = 2
CHIPS_Y = 8

TILE = 256
TILE_ROWS = TILE * TILE // LANES
TILES = (((0, 0), (0, 1), (0, 2), (0, 3), (1, 1)), ((1, 2), (1, 3), (2, 2), (2, 3), (3, 3)))
HALF_ROWS = TILE_ROWS * len(TILES[0])

GROUPS = (("zyx", (0, 1)), ("yzx", (2, 3)), ("xyz", (4,)))


def lane_copy(block, lane):
    return jnp.broadcast_to(block[:, lane:lane + 1], (ROWS, LANES))


def row_copy(block, row):
    return jnp.broadcast_to(block[row:row + 1, :], (ROWS, LANES))


def tree_sum(terms):
    terms = list(terms)
    while len(terms) > 1:
        terms = [sum(terms[i:i + 2][1:], terms[i]) for i in range(0, len(terms), 2)]
    return terms[0]


def factor_panels(gram):
    row = lax.broadcasted_iota(jnp.int32, (ROWS, LANES), 0)
    lane = lax.broadcasted_iota(jnp.int32, (ROWS, LANES), 1)
    panels = RANK // ROWS
    left = [gram[ROWS * p:ROWS * (p + 1), :] for p in range(panels)]
    right = [jnp.where(lane == row + ROWS * p, 1.0, 0.0) for p in range(panels)]
    finished = []
    for p in range(panels):
        diag = [jnp.where(row < ROWS, lane_copy(left[p], ROWS * p + c), 0.0) for c in range(ROWS)]
        scaled = [jnp.zeros((ROWS, LANES), jnp.float32) for _ in range(ROWS)]
        for j in range(ROWS):
            pivot = row_copy(diag[j], j)
            inverse = 1.0 / pivot
            root = lax.rsqrt(pivot)
            at_pivot = row == j
            for c in range(j):
                scaled[c] = jnp.where(at_pivot, diag[c] * root, scaled[c])
            scaled[j] = jnp.where(at_pivot, root, scaled[j])
            column = diag[j]
            for c in range(ROWS):
                if c != j:
                    across = row_copy(diag[c], j) * inverse
                    diag[c] = jnp.where(at_pivot, across, diag[c] - column * across)
            diag[j] = jnp.where(at_pivot, inverse, -column * inverse)
        solved_left = tree_sum(diag[c] * row_copy(left[p], c) for c in range(ROWS))
        solved_right = tree_sum(diag[c] * row_copy(right[p], c) for c in range(ROWS))
        finished.append(tree_sum(scaled[c] * row_copy(right[p], c) for c in range(ROWS)))
        left_rows = [row_copy(solved_left, c) for c in range(ROWS)]
        right_rows = [row_copy(solved_right, c) for c in range(ROWS)]
        later = range(p + 1, panels)
        factors = [[lane_copy(left[q], ROWS * p + c) for q in later] for c in range(ROWS)]
        for number, q in enumerate(later):
            left[q] = left[q] - tree_sum(factors[c][number] * left_rows[c] for c in range(ROWS))
            right[q] = right[q] - tree_sum(factors[c][number] * right_rows[c] for c in range(ROWS))
        yield
    return jnp.concatenate(finished, axis=0)


def inverse_factor(gram):
    panels = factor_panels(gram)
    while True:
        try:
            next(panels)
        except StopIteration as stop:
            return stop.value


def product(left, right):
    return lax.dot_general(left, right, (((1,), (0,)), ((), ())), precision=HIGHEST,
                           preferred_element_type=jnp.float32)


def product_of_rows(left, right):
    return lax.dot_general(left, right, (((1,), (1,)), ((), ())), precision=HIGHEST,
                           preferred_element_type=jnp.float32)


def two_terms(values):
    high = values.astype(jnp.bfloat16)
    return high, (values - high.astype(jnp.float32)).astype(jnp.bfloat16)


def term_product(left, right, contract):
    return lax.dot_general(left, right, ((contract, (0,)), ((), ())), preferred_element_type=jnp.float32)


class Place:
    def __init__(self, chips):
        self.chips = chips
        self.narrow, self.wide = lax.axis_index("narrow"), lax.axis_index("wide")
        self.core = self.narrow % CORES
        self.at = {"z": self.narrow // CORES, "y": self.wide % chips["y"], "x": self.wide // chips["y"]}

    def step(self, axis, offset):
        return (self.at[axis] + offset + self.chips[axis]) % self.chips[axis]

    def device(self, axis, position):
        if axis == "z":
            return (position * CORES + self.core, self.wide)
        if axis == "y":
            return (self.narrow, self.at["x"] * self.chips["y"] + position)
        return (self.narrow, position * self.chips["y"] + self.at["y"])

    def partner(self):
        return (self.narrow + 1 - 2 * self.core, self.wide)

    def along(self, axis):
        return [self.device(axis, self.step(axis, offset)) for offset in range(1, self.chips[axis])]


class Copies:
    def __init__(self, send_sem, recv_sem):
        self.send_sem, self.recv_sem, self.started = send_sem, recv_sem, []

    def start(self, source, target, device):
        index = len(self.started)
        copy = pltpu.make_async_remote_copy(source, target, self.send_sem.at[index], self.recv_sem.at[index],
                                            device_id=device, device_id_type=MESH_ID)
        copy.start()
        self.started.append(copy)
        return copy

    def drain(self):
        for copy in self.started:
            copy.wait_send()


def aligned(start, size):
    return pl.ds(pl.multiple_of(start, ROWS), size)


class Group:
    def __init__(self, chips, axes, tiles):
        self.first, self.second, self.third = axes
        self.tiles = tiles
        self.ring = chips[self.first]
        self.ahead, self.behind = self.ring // 2, (self.ring - 1) // 2
        self.relayed = self.ring == 8
        self.block = TILE_ROWS // self.ring
        self.piece = self.block // chips[self.second]
        self.rows = self.piece * len(tiles)
        self.chips = chips

    def scratch(self):
        def rows(*shape):
            return pltpu.VMEM((*shape, LANES), jnp.float32)

        count, second = len(self.tiles), self.chips[self.second]
        return [rows(count, self.ahead, self.block), rows(count, max(self.behind, 1), self.block),
                rows(second, self.rows), rows(max(second - 1, 1), self.rows),
                rows(self.chips[self.third], self.rows), rows(second, self.rows)]

    def copies(self):
        links = len(self.tiles) * (self.ring - 1)
        return 2 * links + len(self.tiles) * self.ring + 2 * (self.chips[self.second] - 1) + self.chips[self.third] - 1

    def take(self, refs):
        self.up, self.down, self.sums, self.parts, self.slots, self.gathered = refs

    def rows_of(self, tile, position):
        return aligned(tile * TILE_ROWS + position * self.block, self.block)


def start_rows(rows_ref):
    factor = yield from factor_panels(product_of_rows(rows_ref[...], rows_ref[...]))
    rows_ref[...] = product(factor, rows_ref[...])


def hosvd_kernel(chips, field_hbm, start_hbm, out_ref, start_ref, joined, joined_terms, mine, tiles_ref, gram, current,
                 ahead, leaving, cells, split, terms, rows_y, rows_x, load_sem, *rest):
    groups = [Group(chips, axes, tiles) for axes, tiles in GROUPS]
    for number, group in enumerate(groups):
        group.take(rest[6 * number:6 * number + 6])
    copies = Copies(*rest[6 * len(groups):])
    place = Place(chips)
    core = place.core
    devices = CORES * chips["z"]
    others = [(place.narrow + offset) % devices for offset in range(1, devices)]

    barrier = pltpu.get_barrier_semaphore()
    greeted = [(narrow, place.wide) for narrow in others] + place.along("y") + place.along("x")
    for device in greeted:
        pl.semaphore_signal(barrier, inc=1, device_id=device, device_id_type=MESH_ID)
    depth, order_one = field_hbm.shape
    own = aligned(core * depth, depth)
    loads = [pltpu.make_async_copy(field_hbm, joined.at[own, :], load_sem.at[0]),
             pltpu.make_async_copy(start_hbm, start_ref, load_sem.at[1])]
    for load in loads:
        load.start()
    loads[0].wait()
    leaving[...] = jnp.swapaxes(joined[own, :].reshape(ROWS, devices, order_one), 0, 1)
    pl.semaphore_wait(barrier, len(greeted))

    exchange = copies.start(joined.at[own, :], joined.at[own, :], place.partner())
    loads[1].wait()
    current[...] = start_ref[...].T
    starting = start_rows(current)

    def advance(panels):
        for _ in range(panels):
            next(starting, None)

    advance(1)
    exchange.wait_recv()
    for number, term in enumerate(two_terms(joined[...])):
        joined_terms[number] = term

    moving = {}

    def send_ahead(group, tile, source, step):
        device = place.device(group.first, place.step(group.first, 1))
        moving[tile, "up", step] = copies.start(source, group.up.at[group.tiles.index(tile), step], device)

    def send_behind(group, tile, source, step):
        device = place.device(group.first, place.step(group.first, -1))
        moving[tile, "down", step] = copies.start(source, group.down.at[group.tiles.index(tile), step], device)

    def own_block(group, tile, offset):
        return group.rows_of(tile, place.step(group.first, offset))

    def put(group, tile, name, source, target, offset):
        device = place.device(group.first, place.step(group.first, offset))
        moving[tile, name] = copies.start(source, target, device)

    def spread(group, tile):
        index = group.tiles.index(tile)
        for name, target, to, via in (("far", group.up.at[index, 0], -4, -2), ("mid", group.up.at[index, 1], -3, -1),
                                      ("back", group.down.at[index, 0], 3, 1), ("left", group.up.at[index, 2], -1, -1),
                                      ("right", group.down.at[index, 1], 1, 1)):
            put(group, tile, name, mine.at[own_block(group, tile, to), :], target, via)

    def collect(group, tile):
        index = group.tiles.index(tile)
        moving[tile, "far"].wait_recv()
        moving[tile, "mid"].wait_recv()
        group.up[index, 0] = group.up[index, 0] + group.up[index, 1] + mine[own_block(group, tile, -2), :]
        put(group, tile, "up", group.up.at[index, 0], group.up.at[index, 3], -2)
        moving[tile, "back"].wait_recv()
        group.down[index, 0] = group.down[index, 0] + mine[own_block(group, tile, 2), :]
        put(group, tile, "down", group.down.at[index, 0], group.down.at[index, 2], 2)

    def collected(group, tile):
        index = group.tiles.index(tile)
        for name in ("left", "right", "up", "down"):
            moving[tile, name].wait_recv()
        return (mine[own_block(group, tile, 0), :] + group.up[index, 2] + group.down[index, 1] + group.up[index, 3]
                + group.down[index, 2])

    order = [(group, group.tiles[turn]) for turn in range(2) for group in groups if len(group.tiles) == 2]
    order += [(group, tile) for group in groups for tile in group.tiles if len(group.tiles) == 1]
    for group, tile in order:
        rows, columns = (TILES[0][tile][side] + core * (TILES[1][tile][side] - TILES[0][tile][side])
                         for side in range(2))
        row_high, row_low, column_high, column_low = (
            joined_terms[number, :, pl.ds(pl.multiple_of(side * TILE, TILE), TILE)]
            for side in (rows, columns) for number in range(2))
        block = term_product(row_high, column_high, (0,)) + (
            term_product(row_high, column_low, (0,)) + term_product(row_low, column_high, (0,)))
        for half in range(TILE // LANES):
            start = tile * TILE_ROWS + half * TILE
            mine[start:start + TILE, :] = block[:, half * LANES:(half + 1) * LANES]
        if group.relayed:
            spread(group, tile)
            continue
        send_ahead(group, tile, mine.at[group.rows_of(tile, place.step(group.first, group.ahead)), :], 0)
        if group.behind:
            send_behind(group, tile, mine.at[group.rows_of(tile, place.step(group.first, -group.behind)), :], 0)

    pieces = {group: [] for group in groups}

    def keep(group, tile, total):
        index = group.tiles.index(tile)
        for part in range(chips[group.second]):
            group.sums[part, index * group.piece:(index + 1) * group.piece, :] = (
                total[part * group.piece:(part + 1) * group.piece, :])
        if index == len(group.tiles) - 1:
            for offset in range(1, chips[group.second]):
                to = place.step(group.second, offset)
                pieces[group].append(copies.start(group.sums.at[to], group.parts.at[offset - 1],
                                                  place.device(group.second, to)))

    relayed = [(group, tile) for group, tile in order if group.relayed]
    ringed = [(group, tile) for group, tile in order if not group.relayed]
    advance(6)
    for group, tile in relayed:
        collect(group, tile)
    for step in range(1, max(group.ahead for group, _ in ringed) + 1):
        for group, tile in ringed:
            index = group.tiles.index(tile)
            if step < group.ahead:
                moving[tile, "up", step - 1].wait_recv()
                target = place.step(group.first, group.ahead - step)
                group.up[index, step - 1] = group.up[index, step - 1] + mine[group.rows_of(tile, target), :]
                send_ahead(group, tile, group.up.at[index, step - 1], step)
            if step < group.behind:
                moving[tile, "down", step - 1].wait_recv()
                target = place.step(group.first, step - group.behind)
                group.down[index, step - 1] = group.down[index, step - 1] + mine[group.rows_of(tile, target), :]
                send_behind(group, tile, group.down.at[index, step - 1], step)
            if step == group.ahead:
                moving[tile, "up", step - 1].wait_recv()
                total = mine[group.rows_of(tile, place.at[group.first]), :] + group.up[index, step - 1]
                if group.behind:
                    moving[tile, "down", group.behind - 1].wait_recv()
                    total = total + group.down[index, group.behind - 1]
                keep(group, tile, total)
    advance(6)
    for group, tile in relayed:
        keep(group, tile, collected(group, tile))

    arrival = sorted(groups, key=lambda group: group.ahead)
    advance(3)
    for group in arrival:
        total = group.sums[place.at[group.second]]
        for number, copy in enumerate(pieces[group]):
            copy.wait_recv()
            total = total + group.parts[number]
        here = place.at[group.third]
        group.slots[here] = total
        pieces[group] = [copies.start(group.slots.at[here], group.slots.at[here], device)
                         for device in place.along(group.third)]
    advance(RANK)
    for group in arrival:
        for copy in pieces[group]:
            copy.wait_recv()
        total = group.slots[0]
        for slot in range(1, chips[group.third]):
            total = total + group.slots[slot]
        here = place.at[group.second]
        group.gathered[here] = total
        pieces[group] = [copies.start(group.gathered.at[here], group.gathered.at[here], device)
                         for device in place.along(group.second)]

    crossing = {tile: [] for group in groups for tile in group.tiles}

    def cross(tile, rows):
        crossing[tile].append(copies.start(tiles_ref.at[core, rows, :], tiles_ref.at[core, rows, :], place.partner()))

    def pass_on(group, tile, way, step):
        sign = 1 if way == "up" else -1
        rows = group.rows_of(tile, place.step(group.first, -sign * step))
        if way == "up" or step:
            cross(tile, rows)
        if step == (group.ahead if way == "up" else group.behind):
            return
        device = place.device(group.first, place.step(group.first, sign))
        moving[tile, way, step] = copies.start(tiles_ref.at[core, rows, :], tiles_ref.at[core, rows, :], device)

    def hand(group, tile, name, block, offset):
        rows = own_block(group, tile, block)
        put(group, tile, name, tiles_ref.at[core, rows, :], tiles_ref.at[core, rows, :], offset)

    def hand_out(group, tile):
        for offset in (2, -2, 1, -1):
            hand(group, tile, ("own", offset), 0, offset)
        cross(tile, own_block(group, tile, 0))

    def hand_on(group, tile):
        moving[tile, ("own", 2)].wait_recv()
        hand(group, tile, ("next", 2), -2, 2)
        hand(group, tile, ("next", 1), -2, 1)
        moving[tile, ("own", -2)].wait_recv()
        hand(group, tile, ("next", -1), 2, -1)
        moving[tile, ("own", 1)].wait_recv()
        moving[tile, ("own", -1)].wait_recv()
        for block in (-2, 2, -1, 1):
            cross(tile, own_block(group, tile, block))

    def handed(group, tile):
        for offset, block in ((1, -3), (-1, 3), (2, -4)):
            moving[tile, ("next", offset)].wait_recv()
            cross(tile, own_block(group, tile, block))

    for group in arrival:
        for copy in pieces[group]:
            copy.wait_recv()
        for index, tile in enumerate(group.tiles):
            start = tile * TILE_ROWS + place.at[group.first] * group.block
            for part in range(chips[group.second]):
                tiles_ref[core, aligned(start + part * group.piece, group.piece), :] = (
                    group.gathered[part, index * group.piece:(index + 1) * group.piece, :])
            if group.relayed:
                hand_out(group, tile)
                continue
            pass_on(group, tile, "up", 0)
            if group.behind:
                pass_on(group, tile, "down", 0)
    def unpack(side, tile):
        row, column = (pl.multiple_of((TILES[0][tile][way] + side * (TILES[1][tile][way] - TILES[0][tile][way])) * TILE,
                                      TILE) for way in range(2))
        start = tile * TILE_ROWS
        block = jnp.concatenate([tiles_ref[side, start:start + TILE, :],
                                 tiles_ref[side, start + TILE:start + 2 * TILE, :]], axis=1)
        for number, term in enumerate(two_terms(block)):
            gram[number, pl.ds(row, TILE), pl.ds(column, TILE)] = term
        for number, term in enumerate(two_terms(block.T)):
            gram[number, pl.ds(column, TILE), pl.ds(row, TILE)] = term

    def unpack_across(tile):
        for copy in crossing[tile]:
            copy.wait_recv()
        unpack(1 - core, tile)

    for group, tile in relayed:
        hand_on(group, tile)
    for step in range(1, max(group.ahead for group, _ in ringed) + 1):
        for group, tile in ringed:
            if step <= group.ahead:
                moving[tile, "up", step - 1].wait_recv()
                pass_on(group, tile, "up", step)
            if step <= group.behind:
                moving[tile, "down", step - 1].wait_recv()
                pass_on(group, tile, "down", step)
    for group, tile in ringed:
        unpack(core, tile)
    for group, tile in relayed:
        handed(group, tile)
    for group, tile in ringed:
        unpack_across(tile)
    for group, tile in relayed:
        unpack(core, tile)
    for group, tile in relayed:
        unpack_across(tile)

    def regroup(source, target):
        target[place.narrow] = source[place.narrow]
        return [copies.start(source.at[narrow], target.at[place.narrow], (narrow, place.wide)) for narrow in others]

    def sum_along(axis, slots, term):
        slots[place.at[axis]] = term
        here = slots.at[place.at[axis]]
        for copy in [copies.start(here, here, device) for device in place.along(axis)]:
            copy.wait_recv()
        return functools.reduce(lambda total, slot: total + slots[slot], range(1, chips[axis]), slots[0])

    arriving = regroup(leaving, cells)

    def gram_times(rows):
        high, low = two_terms(rows)
        both = term_product(jnp.concatenate([high, low], axis=0), gram[0], (1,))
        ahead[...] = both[:RANK] + (both[RANK:] + term_product(high, gram[1], (1,)))

    gram_times(current[...])
    current[...] = ahead[...]

    def sweep(index, carry):
        rows = current[...]
        factor = inverse_factor(product_of_rows(rows, rows))
        gram_times(rows)
        current[...] = product(factor, ahead[...])
        return carry

    lax.fori_loop(0, ITERS - 1, sweep, 0)
    rows = current[...]
    for copy in arriving:
        copy.wait_recv()
    core_rows = product_of_rows(cells[...].reshape(devices * ROWS, order_one), rows)
    block = product_of_rows(core_rows, inverse_factor(product_of_rows(rows, rows)))
    split[...] = product_of_rows(block, block).reshape(devices, ROWS, devices * ROWS)
    for copy in regroup(split, terms):
        copy.wait_recv()
    total = functools.reduce(lambda total, slot: total + terms[slot], range(1, devices), terms[0])
    out_ref[...] = sum_along("x", rows_x, sum_along("y", rows_y, total))
    copies.drain()


VMEM = pl.BlockSpec(memory_space=pltpu.VMEM)


def mode_two_rows(field_rows, start_block, chips):
    groups = [Group(chips, axes, tiles) for axes, tiles in GROUPS]
    depth, order = field_rows.shape
    devices = CORES * chips["z"]
    width = devices * ROWS
    count = (1 + len(TILES[0]) + sum(group.copies() for group in groups) + 2 * (devices - 1) + chips["y"] + chips["x"]
             - 2)

    def floats(*shape):
        return pltpu.VMEM(shape, jnp.float32)

    def terms(*shape):
        return pltpu.VMEM((2, *shape), jnp.bfloat16)

    return pl.pallas_call(
        functools.partial(hosvd_kernel, chips),
        out_shape=jax.ShapeDtypeStruct((ROWS, width), jnp.float32),
        in_specs=[pl.BlockSpec(memory_space=pl.ANY)] * 2,
        out_specs=VMEM,
        scratch_shapes=[floats(order, RANK), floats(CORES * depth, order), terms(CORES * depth, order),
                        floats(HALF_ROWS, LANES), floats(CORES, HALF_ROWS, LANES), terms(order, order),
                        floats(RANK, order), floats(RANK, order), floats(devices, ROWS, order),
                        floats(devices, ROWS, order), floats(devices, ROWS, width), floats(devices, ROWS, width),
                        floats(chips["y"], ROWS, width), floats(chips["x"], ROWS, width),
                        pltpu.SemaphoreType.DMA((2,))]
        + [shape for group in groups for shape in group.scratch()]
        + [pltpu.SemaphoreType.DMA((count,)), pltpu.SemaphoreType.DMA((count,))],
        compiler_params=pltpu.CompilerParams(collective_id=0, has_side_effects=True, vmem_limit_bytes=48 << 20),
    )(field_rows, start_block)


def shards(chips, field, start_block):
    cells_two, cells_three, order_one = field.shape
    rows = mode_two_rows(field.reshape(cells_two * cells_three, order_one), start_block, chips)
    columns = rows.shape[1] // lax.axis_size("wide")
    finished = lax.dynamic_slice_in_dim(rows, lax.axis_index("wide") * columns, columns, axis=1)
    return finished / (RANK * cells_three * lax.axis_size("wide"))


def solution(mesh, chips_y=CHIPS_Y):
    chips = {"z": mesh.shape["narrow"] // CORES, "y": chips_y, "x": mesh.shape["wide"] // chips_y}
    return jax.shard_map(
        functools.partial(shards, chips),
        mesh=mesh,
        in_specs=(P("narrow", "wide", None), P()),
        out_specs=P("narrow", "wide"),
        check_vma=False,
    )
```
